32 devices in a mesh: section: 2 (over y), expert: 16 (over z, x, core).
Axes of the slice: x: 2, y: 2, z: 4, core: 2. Of those that a mesh axis runs over, the one named last changes fastest.
Arguments:
- inputs: bfloat16 [2, 256, 2560], P('section', 'expert'), may hold values from -6 to 6
- norm_gain: float32 [2, 2, 2560], P(None, 'section'), may hold values from 0.5 to 1.5
- router: bfloat16 [2, 2, 2560, 16], P(None, 'section'), may hold values from -0.125 to 0.125
- w_gate: bfloat16 [2, 2, 16, 2560, 768], P(None, 'section', 'expert'), may hold values from -0.125 to 0.125
- w_up: bfloat16 [2, 2, 16, 2560, 768], P(None, 'section', 'expert'), may hold values from -0.125 to 0.125
- w_down: bfloat16 [2, 2, 16, 768, 2560], P(None, 'section', 'expert'), may hold values from -0.21875 to 0.21875
- routes: int32 [2, 2, 2, 256, 6], P(None, 'section'), may hold values from 0 to 15, all different within a row; in each aligned block of 16 rows (0 to 15, 16 to 31, ..., all dimensions but the last counted through in order) at most 9 rows name the same one
Outputs:
- outputs: bfloat16 [2, 256, 2560], P('section', 'expert')
The draws below stay inside these ranges and needn't reach their ends.
Inputs may be any that keep to these rules, and one draw needn't show every extreme that they name: Each row names 6 different experts. In each aligned block of 16 rows of routes (the tokens of one index of expert in one micro-batch at one layer), no expert is named by more than 9 rows.
All inputs are finite; a program needn't handle non-finite values.
Results may differ from the reference program's by a relative error of at most 0.012.
Values may be sent and summed in bfloat16 or wider, within the bound.
A program may use at most 64 MiB of HBM per device.

```python
import math
import jax
import jax.numpy as jnp
import numpy as np
from jax import lax

D = 2560
H = 768
TOP = 6
LOOPS = 2
SLAB = 16
EXPERTS = 16
TOK_MB = 256
CAP = 9
N_SECTION = 2
N_EXPERT = 16


def steps_of(own_key, shape, cuts, smallest, high):
    def one(dim, blocks):
        draws = jax.random.uniform(jax.random.fold_in(jax.random.fold_in(own_key, 6), dim), (blocks,), jnp.float32, smallest / len(cuts), high / len(cuts))
        return jnp.repeat(jnp.exp(draws), shape[dim] // blocks).reshape((-1,) + (1,) * (len(shape) - dim - 1))

    factor_of = one(*cuts[0])
    for cut in cuts[1:]:
        factor_of = factor_of * one(*cut)
    return factor_of


def routed_block(stream_key, own, number, rows, amount, top, limit, lean):
    ranking = jax.random.permutation(stream_key, amount)
    packed, usual = portions_of(amount, rows * top, limit, lean, True), portions_of(amount, rows * top, limit, lean, False)
    places = jnp.arange(amount)

    def named(sizes, offset_by):
        used = int((sizes > 0).sum())
        fixed = max(1, used // 4)
        passed = fixed + (places - fixed + offset_by * (used - fixed)) % max(1, amount - fixed)
        return jnp.zeros((amount,), jnp.int32).at[ranking[jnp.where(places < fixed, places, passed)]].set(jnp.asarray(sizes, jnp.int32))

    sizes = jnp.where(number % 4 == 0, named(packed, number // 4), named(usual, number - number // 4 - 1))
    mixed = jax.random.permutation(jax.random.fold_in(own, 3), amount)
    source_of, taker = mixed[0:amount // 2 * 2:2], mixed[1:amount // 2 * 2:2]
    margin = jnp.minimum(sizes[source_of] - 1, limit - sizes[taker]) // 2
    margin = jnp.where((source_of == ranking[0]) | (taker == ranking[0]) | (sizes[taker] == 0), 0, jnp.maximum(margin, 0))
    passed = jax.random.randint(jax.random.fold_in(own, 4), (amount // 2,), 0, 1 << 20) % (margin + 1)
    sizes = sizes.at[source_of].add(-passed).at[taker].add(passed)
    members = jnp.searchsorted(jnp.cumsum(sizes), jnp.arange(rows * top), side="right").astype(jnp.int32)
    table = members.reshape(top, rows).T
    table = table[jax.random.permutation(jax.random.fold_in(own, 1), rows)]
    offset_by = jax.random.randint(jax.random.fold_in(own, 2), (rows, 1), 0, top)
    return jnp.take_along_axis(table, (jnp.arange(top)[None, :] + offset_by) % top, axis=1)


def portions_of(amount, total, limit, lean, full):
    loads = [(1 << 20) // math.isqrt(grade ** lean) + 1 for grade in range(1, amount + 1)]
    largest = limit if full else min(limit, max(-(-total // amount), total * loads[0] // sum(loads)))
    least = 1 if total - largest >= amount - 1 else 0
    counts, surplus = [largest] + [least] * (amount - 1), total - largest - least * (amount - 1)
    while surplus > 0:
        movable = [i for i in range(1, amount) if counts[i] < largest] or [i for i in range(1, amount) if counts[i] < limit]
        pool, left = sum([loads[i] for i in movable]), surplus
        for i in movable:
            more = min(limit - counts[i], max(1, left * loads[i] // pool), surplus)
            counts[i] = counts[i] + more
            surplus = surplus - more
    return np.array(counts)


def scatter_about(rng, shape, spread, bound, split=(), held_as=jnp.bfloat16):
    array = jax.random.normal(rng, shape, jnp.float32) * spread
    if len(split) > 0:
        array = steps_of(rng, shape, split, -0.22, 0.18) * array
    return jnp.clip(array, min=-bound, max=bound).astype(held_as)


def setup_inputs(seed: int = 0) -> dict:
    splits = jax.random.split(jax.random.key(seed), 8)
    inputs = scatter_about(splits[0], (N_SECTION, TOK_MB, D), 1.0, 6.0, ((0, 2), (1, 16)))
    norm_gain = jnp.clip(1.0 + 0.1 * jax.random.normal(splits[1], (LOOPS, N_SECTION, D), jnp.float32), 0.5, 1.5)
    router = scatter_about(splits[2], (LOOPS, N_SECTION, D, EXPERTS), D ** -0.5, 0.125, ((1, 2),))
    w_gate = scatter_about(splits[3], (LOOPS, N_SECTION, EXPERTS, D, H), D ** -0.5, 0.125, ((1, 2), (2, 16)))
    w_up = scatter_about(splits[4], (LOOPS, N_SECTION, EXPERTS, D, H), D ** -0.5, 0.125, ((1, 2), (2, 16)))
    w_down = scatter_about(splits[5], (LOOPS, N_SECTION, EXPERTS, H, D), H ** -0.5, 0.21875, ((1, 2), (2, 16)))
    routes_keys = jax.random.split(jax.random.fold_in(splits[6], 1), LOOPS * N_SECTION * N_SECTION * TOK_MB // SLAB)
    routes_turns = jax.random.permutation(jax.random.fold_in(splits[6], 3), LOOPS * N_SECTION * N_SECTION * TOK_MB // SLAB)
    routes = jax.vmap(lambda own, number: routed_block(jax.random.fold_in(splits[6], 2), own, number, SLAB, EXPERTS, TOP, CAP, 1))(routes_keys, routes_turns).reshape((LOOPS, N_SECTION, N_SECTION, TOK_MB, TOP))
    return {"inputs": inputs, "norm_gain": norm_gain, "router": router, "w_gate": w_gate, "w_up": w_up, "w_down": w_down, "routes": routes}


def normalize(values, gain_row):
    wide = values.astype(jnp.float32)
    scale = lax.rsqrt(lax.optimization_barrier(jnp.mean(wide * wide, axis=-1, keepdims=True)) + 1e-06)
    return (wide * scale * gain_row).astype(jnp.bfloat16)

def gate_weights(normed, router_now, routes_rows):
    scores = jnp.dot(normed, router_now, preferred_element_type=jnp.float32)
    expert_ids = jnp.arange(router_now.shape[1], dtype=jnp.int32)
    onehot = (routes_rows[:, :, None] == expert_ids[None, None, :]).astype(jnp.float32)
    picked = lax.optimization_barrier(jnp.sum(onehot * scores[:, None, :], axis=2))
    sigmoid_of = jax.nn.sigmoid(picked)
    return sigmoid_of / lax.optimization_barrier(jnp.sum(sigmoid_of, axis=1, keepdims=True))

def slot_table(routes_rows, slab_rows, experts):
    top_k = routes_rows.shape[1]
    blocks = routes_rows.reshape(-1, slab_rows * top_k)
    expert_ids = jnp.arange(experts, dtype=jnp.int32)
    onehot = (blocks[:, :, None] == expert_ids[None, None, :]).astype(jnp.int32)
    before = jnp.cumsum(onehot, axis=1) - onehot
    return lax.optimization_barrier(jnp.sum(before * onehot, axis=2)).reshape(routes_rows.shape).astype(jnp.int32)

def expert_rows(rows_in, gate_mat, up_mat, down_mat):
    gate_proj = jnp.dot(rows_in, gate_mat, preferred_element_type=jnp.float32)
    up_proj = jnp.dot(rows_in, up_mat, preferred_element_type=jnp.float32)
    hidden = (jax.nn.silu(gate_proj) * up_proj).astype(jnp.bfloat16)
    return jnp.dot(hidden, down_mat, preferred_element_type=jnp.float32).astype(jnp.bfloat16)

def moe_layer(tokens, gain_row, router_now, gate_all, up_all, down_all, routes_rows):
    normed = normalize(tokens, gain_row)
    gates = gate_weights(normed, router_now, routes_rows)
    slots = slot_table(routes_rows, SLAB, EXPERTS)
    source = (jnp.arange(TOK_MB, dtype=jnp.int32) // SLAB)[:, None]
    placed = (routes_rows * N_EXPERT + source) * CAP + slots
    flat_place = placed.reshape(-1).astype(jnp.int32)
    dispatched = jnp.zeros((EXPERTS * N_EXPERT * CAP, D), jnp.bfloat16)
    dispatched = dispatched.at[flat_place].set(jnp.repeat(normed, TOP, axis=0))
    dispatched = dispatched.reshape(EXPERTS, N_EXPERT * CAP, D)
    served = lax.map(lambda item: expert_rows(item[0], item[1], item[2], item[3]), (dispatched, gate_all, up_all, down_all))
    picked = served.reshape(EXPERTS * N_EXPERT * CAP, D)[flat_place].reshape(TOK_MB, TOP, D)
    mixed = lax.optimization_barrier(jnp.sum(gates[:, :, None] * picked.astype(jnp.float32), axis=1))
    return (tokens.astype(jnp.float32) + mixed).astype(jnp.bfloat16)

def reference(inputs, norm_gain, router, w_gate, w_up, w_down, routes):
    current = inputs
    for loop_at in range(LOOPS):

        def one_section(micro_all, params):
            gain_row, router_now, gate_all, up_all, down_all, routes_now = params

            def one_micro(pair):
                return moe_layer(pair[0], gain_row, router_now, gate_all, up_all, down_all, pair[1])
            return (lax.map(one_micro, (micro_all, routes_now)), None)
        current, unused = lax.scan(one_section, current, (norm_gain[loop_at], router[loop_at], w_gate[loop_at], w_up[loop_at], w_down[loop_at], routes[loop_at]))
    return current
```

```python
import functools

import jax
import jax.numpy as jnp
from jax import lax
from jax.experimental import pallas as pl
from jax.experimental.pallas import tpu as pltpu
from jax.sharding import PartitionSpec as P

MESH = pl.DeviceIdType.MESH
F32 = jnp.float32
BF16 = jnp.bfloat16


def relay_kernel(
    sections, zs, parts,
    inp, gain, router, routes, wg_hbm, wu_hbm, wd_hbm,
    out,
    wg, wu, wd, xin, xout, g, hid, gate_col, p, rc, qs, own, rx, ss, rz,
    w_sem, xin_s, xin_r, feed_s, ag_s, ag_r, c_s, c_r, x_s, x_r, z_s, z_r,
):
    slab = inp.shape[1]
    width = inp.shape[2]
    hidden = wg.shape[2]
    experts = 4 * zs
    half = 2 * zs * slab
    quarter = zs * slab
    piece = width // parts
    moments = 2 * sections

    sec = lax.axis_index("section")
    me = lax.axis_index("expert")
    z = lax.div(me, 4)
    x = lax.rem(lax.div(me, 2), 2)
    c = lax.rem(me, 2)
    x_dev = z * 4 + (1 - x) * 2 + c
    c_dev = z * 4 + x * 2 + (1 - c)
    z_at = [lax.rem(z + k, zs) for k in range(1, zs)]
    z_dev = [zk * 4 + x * 2 + c for zk in z_at]

    def weight_copies(loop_at):
        return [
            pltpu.make_async_copy(src.at[loop_at, 0, 0], dst.at[loop_at], w_sem.at[loop_at, k])
            for k, (src, dst) in enumerate(((wg_hbm, wg), (wu_hbm, wu), (wd_hbm, wd)))
        ]

    for loop_at in range(2):
        for copy in weight_copies(loop_at):
            copy.start()

    barrier = pltpu.get_barrier_semaphore()
    for dev in z_dev + [x_dev, c_dev]:
        pl.semaphore_signal(barrier, inc=1, device_id=(sec, dev), device_id_type=MESH)
    for k in range(1, sections):
        pl.semaphore_signal(
            barrier, inc=1, device_id=(lax.rem(sec + k, sections), me), device_id_type=MESH
        )
    pl.semaphore_wait(barrier, zs + 1 + sections - 1)

    def remote(src, dst, s_sem, r_sem, section_to, dev):
        return pltpu.make_async_remote_copy(
            src_ref=src, dst_ref=dst, send_sem=s_sem, recv_sem=r_sem,
            device_id=(section_to, dev), device_id_type=MESH,
        )

    feed = remote(inp.at[0], xin.at[sec], feed_s.at[0], xin_r.at[sec], sec * 0, me)

    @pl.when(sec > 0)
    def _():
        feed.start()

    @pl.when(sec == 0)
    def _():
        xin[0] = inp[0]

    def slab_rows(ref, q):
        return ref.at[pl.ds(pl.multiple_of(q * slab, slab), slab), :]

    def spread(q, k, dev):
        return remote(slab_rows(g, q), slab_rows(g, q), ag_s.at[k], ag_r.at[q], sec, dev)

    def q_of(cc, xx, zz):
        return cc * (2 * zs) + xx * zs + zz

    last = lax.div(sec, sections - 1)

    def hand_over(j):
        upper = lax.div(j, sections)
        to = (1 - last) * (sec + 1) + last * upper * (j - sections)
        slot = j + last * (sections * (1 - upper) + upper * (2 * sections - j))
        return remote(xout.at[j], xin.at[slot], xin_s.at[j], xin_r.at[slot], to, me)

    def step(j, carry):
        loop_at = lax.div(j, sections)
        micro_at = lax.rem(j, sections)

        @pl.when(sec + j > 0)
        def _():
            remote(xout.at[0], xin.at[j], xin_s.at[0], xin_r.at[j], sec, x_dev).wait_recv()

        wide = xin[j].astype(F32)
        scale = lax.rsqrt(jnp.sum(wide * wide, axis=-1, keepdims=True) * (1.0 / width) + 1e-06)
        q_me = q_of(c, x, z)
        g[pl.ds(pl.multiple_of(q_me * slab, slab), slab), :] = (
            wide * scale * gain[loop_at]
        ).astype(BF16)

        sent = []

        def launch(q, dev):
            copy = spread(q, len(sent), dev)
            copy.start()
            sent.append(copy)

        def arrive(q):
            spread(q, 0, x_dev).wait_recv()

        for dev in z_dev:
            launch(q_me, dev)
        launch(q_me, x_dev)
        launch(q_me, c_dev)
        near = [0, zs - 2] + list(range(1, zs - 2))
        for k in near:
            q = q_of(c, x, z_at[k])
            arrive(q)
            launch(q, x_dev)
            launch(q, c_dev)
        for zz in [z] + [z_at[k] for k in near]:
            q = q_of(c, 1 - x, zz)
            arrive(q)
            launch(q, c_dev)
        for xx in (x, 1 - x):
            for zz in [z] + [z_at[k] for k in near]:
                arrive(q_of(1 - c, xx, zz))

        @pl.when(micro_at == 0)
        def _():
            for copy in weight_copies(loop_at):
                copy.wait()

        scores = jnp.dot(g[...], router[loop_at, 0], preferred_element_type=F32)
        lanes = lax.broadcasted_iota(jnp.int32, scores.shape, 1)
        rows = []
        for cc in range(2):
            for xx in range(2):
                for zz in range(zs):
                    i = zz * 4 + xx * 2 + cc
                    rows.append(routes[loop_at, 0, micro_at, i * slab:(i + 1) * slab, :])
        chosen = jnp.concatenate(rows, axis=0)
        hit = chosen[:, 0:1] == lanes
        for k in range(1, routes.shape[4]):
            hit = hit | (chosen[:, k:k + 1] == lanes)
        sig = jnp.where(hit, jax.nn.sigmoid(scores), 0.0)
        mine = jnp.sum(jnp.where(lanes == me, sig, 0.0), axis=1, keepdims=True)
        gate_col[...] = mine / jnp.sum(sig, axis=1, keepdims=True)

        cut = 256
        for h in range(hidden // cut):
            cols = slice(h * cut, (h + 1) * cut)
            gate = jnp.dot(g[...], wg[loop_at, :, cols], preferred_element_type=F32)
            up = jnp.dot(g[...], wu[loop_at, :, cols], preferred_element_type=F32)
            hid[:, cols] = (gate * jax.nn.sigmoid(gate) * up).astype(BF16)

        for copy in sent:
            copy.wait_send()

        def block(ref, start, count, n):
            first = start if isinstance(start, int) else pl.multiple_of(start, slab)
            return ref.at[pl.ds(first, count), pl.ds(n * piece, piece)]

        c_sent, x_sent, z_sent = [], [], []
        for n in range(parts):
            cols = slice(n * piece, (n + 1) * piece)
            down = jnp.dot(hid[...], wd[loop_at, :, cols], preferred_element_type=F32)
            p[:, cols] = (down * gate_col[...]).astype(BF16)
            copy = remote(
                block(p, (1 - c) * half, half, n), block(rc, 0, half, n),
                c_s.at[n], c_r.at[n], sec, c_dev,
            )
            copy.start()
            c_sent.append(copy)
        for n in range(parts):
            c_sent[n].wait_recv()
            away = block(p, c * half + (1 - x) * quarter, quarter, n)[...].astype(F32)
            qs[:, n * piece:(n + 1) * piece] = (
                away + block(rc, (1 - x) * quarter, quarter, n)[...].astype(F32)
            ).astype(BF16)
            copy = remote(
                block(qs, 0, quarter, n), block(rx, 0, quarter, n),
                x_s.at[n], x_r.at[n], sec, x_dev,
            )
            copy.start()
            x_sent.append(copy)
            own[:, n * piece:(n + 1) * piece] = (
                block(p, c * half + x * quarter, quarter, n)[...].astype(F32)
                + block(rc, x * quarter, quarter, n)[...].astype(F32)
            )
        for n in range(parts):
            cols = slice(n * piece, (n + 1) * piece)
            x_sent[n].wait_recv()
            own[:, cols] = own[:, cols] + rx[:, cols].astype(F32)
            ss[:, cols] = own[:, cols].astype(BF16)
            for k in range(zs - 1):
                copy = remote(
                    block(ss, z_at[k] * slab, slab, n), block(rz, k * slab, slab, n),
                    z_s.at[k, n], z_r.at[k, n], sec, z_dev[k],
                )
                copy.start()
                z_sent.append(copy)
        for n in range(parts):
            cols = slice(n * piece, (n + 1) * piece)
            total = block(own, z * slab, slab, n)[...]
            for k in range(zs - 1):
                z_sent[n * (zs - 1) + k].wait_recv()
                total = total + rz[k * slab:(k + 1) * slab, cols].astype(F32)
            xout[j, :, cols] = (xin[j, :, cols].astype(F32) + total).astype(BF16)

        stays = sec + j == (sections - 1) + (moments - 1)

        @pl.when(jnp.logical_not(stays))
        def _():
            hand_over(j).start()

        @pl.when(stays)
        def _():
            xin[moments] = xout[j]

        for copy in c_sent + x_sent + z_sent:
            copy.wait_send()
        return carry

    lax.fori_loop(0, moments, step, 0)

    @pl.when(sec > 0)
    def _():
        feed.wait_send()

    def drain(j, carry):
        @pl.when(sec + j < (sections - 1) + (moments - 1))
        def _():
            hand_over(j).wait_send()
        return carry

    lax.fori_loop(0, moments, drain, 0)

    @pl.when(sec < sections - 1)
    def _():
        remote(
            xout.at[0], xin.at[moments], xin_s.at[0], xin_r.at[moments], sec, x_dev
        ).wait_recv()

    out[0] = xin[moments]


def per_device(inputs, norm_gain, router, w_gate, w_up, w_down, routes):
    sections = lax.axis_size("section")
    experts = lax.axis_size("expert")
    zs = experts // 4
    slab = inputs.shape[1]
    width = inputs.shape[2]
    hidden = w_gate.shape[4]
    tokens = experts * slab
    parts = 5
    moments = 2 * sections
    vmem = pl.BlockSpec(memory_space=pltpu.VMEM)
    anywhere = pl.BlockSpec(memory_space=pl.ANY)
    dma = pltpu.SemaphoreType.DMA
    return pl.pallas_call(
        functools.partial(relay_kernel, sections, zs, parts),
        out_shape=jax.ShapeDtypeStruct(inputs.shape, inputs.dtype),
        in_specs=[vmem] * 4 + [anywhere] * 3,
        out_specs=vmem,
        scratch_shapes=[
            pltpu.VMEM((2, width, hidden), BF16),
            pltpu.VMEM((2, width, hidden), BF16),
            pltpu.VMEM((2, hidden, width), BF16),
            pltpu.VMEM((moments + 1, slab, width), BF16),
            pltpu.VMEM((moments, slab, width), BF16),
            pltpu.VMEM((tokens, width), BF16),
            pltpu.VMEM((tokens, hidden), BF16),
            pltpu.VMEM((tokens, 1), F32),
            pltpu.VMEM((tokens, width), BF16),
            pltpu.VMEM((tokens // 2, width), BF16),
            pltpu.VMEM((tokens // 4, width), BF16),
            pltpu.VMEM((tokens // 4, width), F32),
            pltpu.VMEM((tokens // 4, width), BF16),
            pltpu.VMEM((tokens // 4, width), BF16),
            pltpu.VMEM(((zs - 1) * slab, width), BF16),
            dma((2, 3)),
            dma((moments,)),
            dma((moments + 1,)),
            dma((1,)),
            dma((experts - 1,)),
            dma((experts,)),
            dma((parts,)),
            dma((parts,)),
            dma((parts,)),
            dma((parts,)),
            dma((zs - 1, parts)),
            dma((zs - 1, parts)),
        ],
        compiler_params=pltpu.CompilerParams(
            collective_id=0, has_side_effects=True, vmem_limit_bytes=56 * 1024 * 1024
        ),
    )(inputs, norm_gain, router, routes, w_gate, w_up, w_down)


def solution(mesh):
    return jax.shard_map(
        per_device,
        mesh=mesh,
        in_specs=(
            P("section", "expert", None),
            P(None, "section", None),
            P(None, "section", None, None),
            P(None, "section", "expert", None, None),
            P(None, "section", "expert", None, None),
            P(None, "section", "expert", None, None),
            P(None, "section", None, None, None),
        ),
        out_specs=P("section", "expert", None),
        check_vma=False,
    )
```
